32 devices in a mesh: group: 2 (over x), tm: 4 (over y, core), inline: 4 (over z).
Axes of the slice: x: 2, y: 2, z: 4, core: 2. Of those that a mesh axis runs over, the one named last changes fastest.
Arguments:
- near_trace: float32 [128, 512], P(('group', 'inline'), 'tm'), parts along dimension 0, may hold values from -1.5 to 1.5
- far_trace: float32 [128, 512], P(('group', 'inline'), 'tm'), parts along dimension 0, may hold values from -1.5 to 1.5
- inline_weight: int32 [128, 512], P(('group', 'inline'), 'tm'), parts along dimension 0, may hold values from 0 to 15
- time_weight: int32 [128, 512], P(('group', 'inline'), 'tm'), parts along dimension 0, may hold values from 0 to 15
- lag_low: int32 [128], P(('group', 'inline')), parts along dimension 0, may hold values from 0 to 15
- lag_high: int32 [128], P(('group', 'inline')), parts along dimension 0, may hold values from 48 to 63
- strain: int32 [16], P(('group', 'tm')), parts along dimension 0, may hold values from 1 to 3
Outputs:
- accumulated: float32 [64, 128, 512], P(None, ('group', 'inline'), 'tm'), parts along dimension 1
The draws below stay inside these ranges and needn't reach their ends.
There are 2 independent parts, one for each index of `group`. The reference program is written for one: setup_inputs(seed, part) draws one part's arguments, and reference() takes and returns one part's arrays. A program takes and returns all parts, laid end to end along the dimension named above; each array names one. Nothing has to cross between parts.
All inputs are finite; a program needn't handle non-finite values.
Results may differ from the reference program's by a relative error of at most 0.0003.
Values sent between devices are 32-bit elements; how exact they have to be, the bound alone decides.
A program may use at most 64 MiB of HBM per device.

```python
import math
import jax
import jax.numpy as jnp
from jax import lax

L = 64
STRETCH = 64
ITERS = 10
NTR = 64
NS = 512
NCHUNK = 8


def survey_pair(key):
    subkeys = jax.random.split(jax.random.fold_in(key, 7321), 6)
    period = jax.random.uniform(subkeys[0], (NTR, 1), jnp.float32, 12.0, 20.0)
    phase_shift = jax.random.uniform(subkeys[1], (NTR, 1), jnp.float32, 0.0, 1.0)
    delay_lags = jax.random.uniform(subkeys[2], (NTR, 1), jnp.float32, 0.0, 16.0)
    samples = jnp.arange(NS, dtype=jnp.float32)[None, :]
    amplitude = jax.random.uniform(subkeys[3], (NTR, 1), jnp.float32, 0.7, 1.3)
    near_noise = 0.06 * jax.random.truncated_normal(subkeys[4], -3.0, 3.0, (NTR, NS), jnp.float32)
    far_noise = 0.06 * jax.random.truncated_normal(subkeys[5], -3.0, 3.0, (NTR, NS), jnp.float32)
    near_angle = 2.0 * math.pi * (jnp.mod(samples, period) / period + phase_shift)
    far_angle = 2.0 * math.pi * (jnp.mod(samples - delay_lags, period) / period + phase_shift)
    near_values = amplitude * jnp.cos(near_angle) + near_noise
    far_values = amplitude * jnp.cos(far_angle) + far_noise
    return (jnp.clip(near_values, -1.5, 1.5), jnp.clip(far_values, -1.5, 1.5))


def draw_near_trace(key, part):
    return survey_pair(key)[0].astype(jnp.float32)


def draw_far_trace(key, part):
    return survey_pair(key)[1].astype(jnp.float32)


def place_ends(values, own_key, least, top_value):
    spot = [jax.random.randint(jax.random.fold_in(own_key, axis), (), 0, length) for axis, length in enumerate(values.shape)]
    longest = values.shape.index(max(values.shape))
    neighbour = spot[:longest] + [(spot[longest] + 1) % values.shape[longest]] + spot[longest + 1:]
    return values.at[tuple(spot)].set(least).at[tuple(neighbour)].set(top_value)


def setup_inputs(seed: int = 0, part: int = 0) -> dict:
    seeds = jax.random.split(jax.random.key(seed), 8)
    own_keys = jax.random.split(jax.random.fold_in(seeds[7], part), 8)
    near_trace = draw_near_trace(jax.random.fold_in(jax.random.fold_in(seeds[7], part), 71), part)
    far_trace = draw_far_trace(jax.random.fold_in(jax.random.fold_in(seeds[7], part), 71), part)
    inline_weight = place_ends(jax.random.randint(own_keys[2], (NTR, NS), 0, 16), jax.random.fold_in(own_keys[2], 1), 0, 15).astype(jnp.int32)
    time_weight = place_ends(jax.random.randint(own_keys[3], (NTR, NS), 0, 16), jax.random.fold_in(own_keys[3], 1), 0, 15).astype(jnp.int32)
    lag_low = place_ends(jax.random.randint(own_keys[4], (NTR,), 0, 16), jax.random.fold_in(own_keys[4], 1), 0, 15).astype(jnp.int32)
    lag_high = place_ends(jax.random.randint(own_keys[5], (NTR,), 48, 64), jax.random.fold_in(own_keys[5], 1), 48, 63).astype(jnp.int32)
    strain = place_ends(jax.random.randint(own_keys[6], (NCHUNK,), 1, 4), jax.random.fold_in(own_keys[6], 1), 1, 3).astype(jnp.int32)
    return dict(near_trace=near_trace, far_trace=far_trace, inline_weight=inline_weight, time_weight=time_weight, lag_low=lag_low, lag_high=lag_high, strain=strain)


BIG = 1.0e9
PENALTY = 2.0
FACE_SCALE = 0.016


def min_filter(values, radius):
    width_count = values.shape[-1]
    rim_fill = jnp.full(values.shape[:-1] + (3,), BIG, jnp.float32)
    extended = jnp.concatenate([rim_fill, values, rim_fill], axis=-1)
    result = values
    for shift_step in (1, 2, 3):
        candidate = jnp.minimum(extended[..., 3 + shift_step:3 + shift_step + width_count], extended[..., 3 - shift_step:3 - shift_step + width_count])
        result = jnp.where(shift_step <= radius, jnp.minimum(result, candidate), result)
    return result


def smooth(volume, inline_pad, time_pad):
    inline_face = FACE_SCALE * jnp.minimum(inline_pad[:-1, :], inline_pad[1:, :])[:, 1:-1]
    inline_flux = inline_face * (volume[:, 1:, 1:-1] - volume[:, :-1, 1:-1])
    time_face = FACE_SCALE * jnp.minimum(time_pad[:, :-1], time_pad[:, 1:])[1:-1, :]
    time_flux = time_face * (volume[:, 1:-1, 1:] - volume[:, 1:-1, :-1])
    centre_cells = volume[:, 1:-1, 1:-1]
    return centre_cells + inline_flux[:, 1:, :] - inline_flux[:, :-1, :] + time_flux[:, :, 1:] - time_flux[:, :, :-1]


def reference(near_trace, far_trace, inline_weight, time_weight, lag_low, lag_high, strain):
    trace_count, sample_count = near_trace.shape
    half_lags = L // 2
    padded_far = jnp.pad(far_trace, ((0, 0), (half_lags, half_lags)))
    shifted = jnp.stack([padded_far[:, lag_shift:lag_shift + sample_count] for lag_shift in range(L)])
    misfit = jnp.square(near_trace[None] - shifted)
    lag_index = lax.broadcasted_iota(jnp.int32, (L, trace_count, 1), 0)
    outside = (lag_index < lag_low[None, :, None]) | (lag_index > lag_high[None, :, None])
    misfit = misfit + PENALTY * outside.astype(jnp.float32)
    inline_pad = jnp.pad(inline_weight.astype(jnp.float32), 1)
    time_pad = jnp.pad(time_weight.astype(jnp.float32), 1)
    for sweep_index in range(ITERS):
        misfit = smooth(jnp.pad(misfit, ((0, 0), (1, 1), (1, 1))), inline_pad, time_pad)
    radius_all = jnp.repeat(strain, STRETCH, total_repeat_length=sample_count)
    sequence = jnp.transpose(misfit, (2, 1, 0))

    def advance(carried, inputs):
        sample, radius = inputs
        updated = sample + min_filter(carried, radius)
        return updated, updated

    start = jnp.zeros((trace_count, L), jnp.float32)
    unused, history = lax.scan(advance, start, (sequence, radius_all))
    history = history - jnp.min(history, axis=-1, keepdims=True)
    return jnp.transpose(history, (2, 1, 0))
```

```python
import functools

import jax
import jax.numpy as jnp
from jax import lax
from jax.experimental import pallas as pl
from jax.experimental.pallas import tpu as pltpu
from jax.sharding import PartitionSpec as P

L = 64
STRETCH = 64
ITERS = 10

BIG = 1000000000.0
PENALTY = 2.0
FACE_SCALE = 0.016

SUB = 8
LANES = 128
GROUPS = L // SUB
HALF = L // 2
REACH = ITERS
PITCH = LANES // GROUPS
SHIFTS = 3

OFFSETS = [(di, dj) for di in (-1, 0, 1) for dj in (-1, 0, 1) if (di, dj) != (0, 0)]


def slot_of(di, dj):
    return (di + 1) * 3 + dj + 1


def roll(x, shift, axis=1):
    shift %= x.shape[axis]
    return pltpu.roll(x, shift, axis) if shift else x


def kernel(
    dims,
    far_in,
    near_in,
    inline_in,
    time_in,
    low_in,
    high_in,
    strain_in,
    y_ref,
    trace_ref,
    weight_ref,
    trace_recv,
    weight_recv,
    plain_ref,
    field_ref,
    face_ref,
    far_ref,
    bound_ref,
    m_ref,
    packed_ref,
    loose_ref,
    enter_ref,
    low_ref,
    high_ref,
    strain_ref,
    local_sems,
    send_sems,
    recv_sems,
    send_sem,
    recv_sem,
):
    rows, width, count, count_in, tall, high, chunk, deep = dims
    me = lax.axis_index("tm")
    here_in = lax.axis_index("inline")

    def present(di, dj):
        ok = None
        for step, place, total in ((di, here_in, count_in), (dj, me, count)):
            if step:
                inside = (place + step >= 0) & (place + step < total)
                ok = inside if ok is None else ok & inside
        return ok

    def device(di, dj):
        return {
            "inline": lax.clamp(0, here_in + di, count_in - 1),
            "tm": lax.clamp(0, me + dj, count - 1),
        }

    local = [
        pltpu.make_async_copy(source, target, local_sems.at[k])
        for k, (source, target) in enumerate(
            (
                (far_in, trace_ref.at[0]),
                (near_in, trace_ref.at[1]),
                (inline_in, weight_ref.at[0]),
                (time_in, weight_ref.at[1]),
                (low_in, low_ref),
                (high_in, high_ref),
                (strain_in, strain_ref),
            )
        )
    ]
    for copy in local:
        copy.start()

    line = lax.broadcasted_iota(jnp.int32, (1, LANES), 1)
    barrier = pltpu.get_barrier_semaphore()
    for di, dj in OFFSETS:

        @pl.when(present(di, dj))
        def _():
            pl.semaphore_signal(
                barrier, inc=1, device_id=device(di, dj), device_id_type=pl.DeviceIdType.MESH
            )

    beside = [
        1 + (place > 0).astype(jnp.int32) + (place < total - 1).astype(jnp.int32)
        for place, total in ((here_in, count_in), (me, count))
    ]
    for copy in local:
        copy.wait()
    for r in range(rows):
        weight_ref[2, r : r + 1, :] = jnp.where(line < LANES // 2, low_ref[r], -high_ref[r])

    pl.semaphore_wait(barrier, beside[0] * beside[1] - 1)

    def part(di):
        return {-1: slice(0, REACH), 0: slice(0, rows), 1: slice(rows - REACH, rows)}[di]

    def halo_copies(di, dj):
        target = slot_of(-di, -dj)
        cut = part(di)
        planes = 3 if dj == 0 else 2
        return [
            pltpu.make_async_remote_copy(
                src_ref=source.at[0:depth, cut, :],
                dst_ref=landing.at[target, 0:depth, cut, :],
                send_sem=send_sems.at[kind, slot_of(di, dj)],
                recv_sem=recv_sems.at[kind, target],
                device_id=device(di, dj),
                device_id_type=pl.DeviceIdType.MESH,
            )
            for kind, (source, landing, depth) in enumerate(
                ((trace_ref, trace_recv, 2), (weight_ref, weight_recv, planes))
            )
        ]

    for di, dj in OFFSETS:

        @pl.when(present(di, dj))
        def _():
            for copy in halo_copies(di, dj):
                copy.start()

        @pl.when(jnp.logical_not(present(di, dj)))
        def _():
            trace_recv[slot_of(di, dj)] = jnp.zeros(trace_ref.shape, jnp.float32)
            weight_recv[slot_of(di, dj)] = jnp.zeros(weight_ref.shape, jnp.int32)

    for di, dj in OFFSETS:

        @pl.when(present(di, dj))
        def _():
            for copy in halo_copies(-di, -dj):
                copy.wait_recv()

    def cells(field, di, dj):
        cut = part(-di)
        own_ref, landing = (trace_ref, trace_recv) if field < 2 else (weight_ref, weight_recv)
        plane = field % 2 if field < 4 else 2
        if di == 0 and dj == 0:
            x = own_ref[plane, cut, :]
        else:
            x = landing[slot_of(di, dj), plane, cut, :]
        return x.astype(jnp.float32)

    def windows(field, di, before):
        left, own, right = (cells(field, di, dj) for dj in (-1, 0, 1))
        first = roll(jnp.where(line >= width - before, left, own), before)
        second = roll(jnp.where(line >= width - before, own, right), before)
        return first, second

    def ahead_by(first, second, k):
        if k == 0:
            return first, second
        return roll(jnp.where(line < k, second, first), -k), roll(second, -k)

    tops = {-1: 0, 0: REACH, 1: REACH + rows}
    for di in (-1, 0, 1):
        top = tops[di]
        size = REACH if di else rows
        pair = windows(0, di, REACH + HALF)
        for k in range(SHIFTS):
            for tile, x in enumerate(ahead_by(*pair, k)):
                plain_ref[1, tile, k * high + top : k * high + top + size, :] = x
        for tile, x in enumerate(windows(1, di, REACH)):
            plain_ref[0, tile, top : top + size, :] = x
        for tile, x in enumerate(windows(2, di, REACH)):
            plain_ref[2, tile, top : top + size, :] = x
        pair = windows(3, di, REACH)
        for tile, (x, y) in enumerate(zip(pair, ahead_by(*pair, 1))):
            plain_ref[0, tile, 2 * high + top : 2 * high + top + size, :] = (
                FACE_SCALE * jnp.minimum(x, y)
            )
        bound_ref[top : top + size, :] = cells(4, di, 0)
    for tile in range(2):
        plain_ref[0, tile, high : high + tall - 1, :] = FACE_SCALE * jnp.minimum(
            plain_ref[2, tile, 0 : tall - 1, :], plain_ref[2, tile, 1:tall, :]
        )
    for kind in range(2):
        for tile in range(2):
            field_ref[kind, tile * LANES : (tile + 1) * LANES, :] = jnp.transpose(
                plain_ref[kind, tile]
            )
    for c in range(chunk):
        part_c = field_ref[0, pl.ds(c, PITCH, stride=chunk), :]
        face_ref[c] = jnp.transpose(jnp.concatenate([part_c] * GROUPS, axis=0))
    for y in range(0, chunk + SUB - 1, SHIFTS):
        parts = [
            field_ref[1, pl.ds(y + g * SUB, PITCH, stride=chunk), :] for g in range(GROUPS)
        ]
        block = jnp.transpose(jnp.concatenate(parts, axis=0))
        for k in range(SHIFTS):
            if y + k < deep:
                far_ref[pl.ds(y + k, tall, stride=deep), :] = block[
                    k * high : k * high + tall
                ]

    sub = lax.broadcasted_iota(jnp.int32, (SUB, LANES), 0)
    lane = lax.broadcasted_iota(jnp.int32, (SUB, LANES), 1)
    lag = ((lane // PITCH) * SUB + sub).astype(jnp.float32)
    key = jnp.where(lane < LANES // 2, lag, -lag)

    def build(t, carry):
        penalty = jnp.where(key < bound_ref[pl.ds(t, 1), :], PENALTY, 0.0)
        for c in range(chunk):
            near = face_ref[c, pl.ds(t, 1), :]
            diff = near - far_ref[pl.ds(t * deep + c, SUB), :]
            m_ref[t, c] = diff * diff + penalty
        return carry

    lax.fori_loop(0, tall, build, 0, unroll=4)

    for step in range(1, ITERS + 1):
        start, stop = step, tall - step

        def relax(t, state):
            here, before = state
            along = []
            for c in range(chunk):
                after = here[c + 1] if c < chunk - 1 else pltpu.roll(here[0], LANES - 1, 1)
                along.append(face_ref[c, pl.ds(2 * high + t, 1), :] * (after - here[c]))
            back = [pltpu.roll(along[-1], 1, 1)] + along[:-1]
            nexts, fluxes = [], []
            for c in range(chunk):
                ahead = m_ref[t + 1, c]
                across = face_ref[c, pl.ds(high + t, 1), :] * (ahead - here[c])
                m_ref[t, c] = (here[c] + (across - before[c])) + (along[c] - back[c])
                nexts.append(ahead)
                fluxes.append(across)
            return nexts, fluxes

        here = [m_ref[start, c] for c in range(chunk)]
        before = [
            face_ref[c, high + start - 1 : high + start, :] * (here[c] - m_ref[start - 1, c])
            for c in range(chunk)
        ]
        lax.fori_loop(start, stop, relax, (here, before), unroll=stop - start)

    for c in range(chunk):
        block = m_ref[REACH : REACH + rows, c].reshape(LANES, LANES)
        packed_ref[c * LANES : (c + 1) * LANES, :] = jnp.transpose(block)

    def unpack(x):
        return [roll(x, -v) for v in range(GROUPS)]

    spots = [lane % GROUPS == v for v in range(GROUPS)]

    def pack(xs):
        result = xs[0]
        for v in range(1, GROUPS):
            result = jnp.where(spots[v], roll(xs[v], v), result)
        return result

    def loose(index):
        return pl.ds(pl.multiple_of(index * SUB, SUB), SUB)

    @pl.when(me > 0)
    def _():
        def loosen(i, carry):
            for c in range(chunk):
                x = packed_ref[pl.ds(c * LANES + i, SUB, stride=PITCH), :]
                for v, y in enumerate(unpack(x)):
                    loose_ref[loose((i * chunk + c) * GROUPS + v), :] = y
            return carry

        lax.fori_loop(REACH // chunk, (width + REACH - 1) // chunk + 1, loosen, 0)

    last = width - 1
    state_copy = pltpu.make_async_remote_copy(
        src_ref=y_ref.at[last * SUB : (last + 1) * SUB, :],
        dst_ref=enter_ref,
        send_sem=send_sem,
        recv_sem=recv_sem,
        device_id={"tm": lax.min(me + 1, count - 1)},
        device_id_type=pl.DeviceIdType.MESH,
    )

    at_low = sub == 0
    at_high = sub == SUB - 1
    top = GROUPS - 1
    wide3 = [strain_ref[k] >= 3 for k in range(width // STRETCH)]
    wide2 = [strain_ref[k] >= 2 for k in range(width // STRETCH)]

    def advance(x, cost, k):
        wide = {v: x[v] for v in range(GROUPS)}
        for d in range(1, 4):
            wide[-d] = jnp.where(at_low, BIG, pltpu.roll(x[GROUPS - d], 1, 0))
            wide[top + d] = jnp.where(at_high, BIG, pltpu.roll(x[d - 1], SUB - 1, 0))
        pair = {v: jnp.minimum(wide[v], wide[v + 1]) for v in range(-1, GROUPS)}
        gate2 = jnp.full((SUB, LANES), jnp.where(wide2[k], -BIG, BIG), jnp.float32)
        gate3 = jnp.full((SUB, LANES), jnp.where(wide3[k], -BIG, BIG), jnp.float32)
        result = []
        for v in range(GROUPS):
            near3 = jnp.minimum(pair[v - 1], pair[v])
            two = jnp.maximum(jnp.minimum(wide[v - 2], wide[v + 2]), gate2)
            three = jnp.maximum(jnp.minimum(wide[v - 3], wide[v + 3]), gate3)
            result.append(cost[v] + jnp.minimum(near3, jnp.minimum(two, three)))
        return result

    @pl.when(me == 0)
    def _():
        state = [jnp.zeros((SUB, LANES), jnp.float32)] * GROUPS
        for s in range(width):
            x = s + REACH
            cost = unpack(packed_ref[pl.ds((x % chunk) * LANES + x // chunk, SUB, stride=PITCH), :])
            state = advance(state, cost, s // STRETCH)
            if s < last:
                for v in range(GROUPS):
                    loose_ref[loose(s * GROUPS + v), :] = state[v]
        y_ref[last * SUB : (last + 1) * SUB, :] = pack(state)

    @pl.when(me > 0)
    def _():
        state_copy.wait_recv()
        state = unpack(enter_ref[...])
        for s in range(width):
            cost = [loose_ref[loose((s + REACH) * GROUPS + v), :] for v in range(GROUPS)]
            state = advance(state, cost, s // STRETCH)
            y_ref[s * SUB : (s + 1) * SUB, :] = pack(state)

    @pl.when(me < count - 1)
    def _():
        state_copy.start()

    @pl.when(me == 0)
    def _():
        def tighten(s, carry):
            x = [loose_ref[loose(s * GROUPS + v), :] for v in range(GROUPS)]
            y_ref[pl.ds(pl.multiple_of(s * SUB, SUB), SUB), :] = pack(x)
            return carry

        lax.fori_loop(0, last, tighten, 0, unroll=4)

    @pl.when(me < count - 1)
    def _():
        state_copy.wait_send()

    for di, dj in OFFSETS:

        @pl.when(present(di, dj))
        def _():
            for copy in halo_copies(di, dj):
                copy.wait_send()


def spread(dims, y_ref, out_ref, turned_ref):
    rows, width = dims
    least = [None] * rows
    for g in range(SUB):
        block = jnp.transpose(y_ref[pl.ds(g, width, stride=SUB), :])
        turned_ref[g] = block
        for r in range(rows):
            tile = block[r * SUB : (r + 1) * SUB]
            least[r] = tile if g == 0 else jnp.minimum(least[r], tile)
    for r in range(rows):
        low = jnp.min(least[r], axis=0, keepdims=True)
        for g in range(SUB):
            tile = turned_ref[g, r * SUB : (r + 1) * SUB, :] - low
            out_ref[pl.ds(g * SUB * rows + r, SUB, stride=rows), :] = tile


def per_device(near_trace, far_trace, inline_weight, time_weight, lag_low, lag_high, strain):
    rows, width = near_trace.shape
    count = lax.axis_size("tm")
    count_in = lax.axis_size("inline")
    tall = rows + 2 * REACH
    high = -(-tall // SUB) * SUB
    chunk = -(-(width + 2 * REACH) // PITCH)
    deep = -(-(chunk + SUB - 1) // SUB) * SUB
    assert width == LANES and rows * SUB == LANES and SHIFTS * high <= LANES
    assert chunk * PITCH + L <= 2 * LANES and REACH + HALF <= width
    vmem = pl.BlockSpec(memory_space=pltpu.VMEM)
    packed = pl.pallas_call(
        functools.partial(kernel, (rows, width, count, count_in, tall, high, chunk, deep)),
        out_shape=jax.ShapeDtypeStruct((width * SUB, LANES), jnp.float32),
        in_specs=[pl.BlockSpec(memory_space=pltpu.HBM)] * 7,
        out_specs=vmem,
        scratch_shapes=[
            pltpu.VMEM((2, rows, width), jnp.float32),
            pltpu.VMEM((3, rows, width), jnp.int32),
            pltpu.VMEM((9, 2, rows, width), jnp.float32),
            pltpu.VMEM((9, 3, rows, width), jnp.int32),
            pltpu.VMEM((3, 2, LANES, LANES), jnp.float32),
            pltpu.VMEM((2, 2 * LANES, LANES), jnp.float32),
            pltpu.VMEM((chunk, LANES, LANES), jnp.float32),
            pltpu.VMEM((tall * deep, LANES), jnp.float32),
            pltpu.VMEM((high, LANES), jnp.float32),
            pltpu.VMEM((tall, chunk, SUB, LANES), jnp.float32),
            pltpu.VMEM((chunk * LANES, LANES), jnp.float32),
            pltpu.VMEM((chunk * PITCH * GROUPS * SUB, LANES), jnp.float32),
            pltpu.VMEM((SUB, LANES), jnp.float32),
            pltpu.SMEM(lag_low.shape, jnp.int32),
            pltpu.SMEM(lag_high.shape, jnp.int32),
            pltpu.SMEM(strain.shape, jnp.int32),
            pltpu.SemaphoreType.DMA((7,)),
            pltpu.SemaphoreType.DMA((2, 9)),
            pltpu.SemaphoreType.DMA((2, 9)),
            pltpu.SemaphoreType.DMA,
            pltpu.SemaphoreType.DMA,
        ],
        compiler_params=pltpu.CompilerParams(
            collective_id=0, has_side_effects=True, vmem_limit_bytes=24 << 20
        ),
    )(
        *[
            pltpu.with_memory_space_constraint(x, pltpu.HBM)
            for x in (far_trace, near_trace, inline_weight, time_weight, lag_low, lag_high, strain)
        ]
    )
    out = pl.pallas_call(
        functools.partial(spread, (rows, width)),
        out_shape=jax.ShapeDtypeStruct((L * rows, width), jnp.float32),
        in_specs=[vmem],
        out_specs=vmem,
        scratch_shapes=[pltpu.VMEM((SUB, LANES, width), jnp.float32)],
        compiler_params=pltpu.CompilerParams(vmem_limit_bytes=24 << 20),
    )(packed)
    return out.reshape(L, rows, width)


def solution(mesh):
    return jax.shard_map(
        per_device,
        mesh=mesh,
        in_specs=(
            P(("group", "inline"), "tm"),
            P(("group", "inline"), "tm"),
            P(("group", "inline"), "tm"),
            P(("group", "inline"), "tm"),
            P(("group", "inline")),
            P(("group", "inline")),
            P(("group", "tm")),
        ),
        out_specs=P(None, ("group", "inline"), "tm"),
        check_vma=False,
    )
```

```python
import functools

import jax
import jax.numpy as jnp
from jax import lax
from jax.experimental import pallas as pl
from jax.experimental.pallas import tpu as pltpu
from jax.sharding import PartitionSpec as P

L = 64
STRETCH = 64
ITERS = 10

BIG = 1000000000.0
PENALTY = 2.0
FACE_SCALE = 0.016

SUB = 8
LANES = 128
GROUPS = L // SUB
HALF = L // 2
REACH = ITERS
PITCH = LANES // GROUPS
SHIFTS = 3

OFFSETS = [(di, dj) for di in (-1, 0, 1) for dj in (-1, 0, 1) if (di, dj) != (0, 0)]


def slot_of(di, dj):
    return (di + 1) * 3 + dj + 1


def roll(x, shift, axis=1):
    shift %= x.shape[axis]
    return pltpu.roll(x, shift, axis) if shift else x


def kernel(
    dims,
    far_in,
    near_in,
    inline_in,
    time_in,
    low_in,
    high_in,
    strain_in,
    y_ref,
    trace_ref,
    weight_ref,
    pack_ref,
    trace_recv,
    weight_recv,
    pack_recv,
    plain_ref,
    inline_ref,
    field_ref,
    face_ref,
    far_ref,
    bound_ref,
    m_ref,
    packed_ref,
    loose_ref,
    enter_ref,
    low_ref,
    high_ref,
    strain_ref,
    local_sems,
    send_sems,
    recv_sems,
    send_sem,
    recv_sem,
):
    rows, width, count, count_in, tall, high, chunk, deep = dims
    edge = REACH + HALF
    filled = edge + 3 * REACH
    me = lax.axis_index("tm")
    here_in = lax.axis_index("inline")

    def present(di, dj):
        ok = None
        for step, place, total in ((di, here_in, count_in), (dj, me, count)):
            if step:
                inside = (place + step >= 0) & (place + step < total)
                ok = inside if ok is None else ok & inside
        return ok

    def device(di, dj):
        return {
            "inline": lax.clamp(0, here_in + di, count_in - 1),
            "tm": lax.clamp(0, me + dj, count - 1),
        }

    local = [
        pltpu.make_async_copy(source, target, local_sems.at[k])
        for k, (source, target) in enumerate(
            (
                (far_in, trace_ref.at[0]),
                (near_in, trace_ref.at[1]),
                (inline_in, weight_ref.at[0]),
                (time_in, weight_ref.at[1]),
                (low_in, low_ref),
                (high_in, high_ref),
                (strain_in, strain_ref),
            )
        )
    ]
    for copy in local:
        copy.start()

    line = lax.broadcasted_iota(jnp.int32, (1, LANES), 1)
    barrier = pltpu.get_barrier_semaphore()
    for di, dj in OFFSETS:

        @pl.when(present(di, dj))
        def _():
            pl.semaphore_signal(
                barrier, inc=1, device_id=device(di, dj), device_id_type=pl.DeviceIdType.MESH
            )

    beside = [
        1 + (place > 0).astype(jnp.int32) + (place < total - 1).astype(jnp.int32)
        for place, total in ((here_in, count_in), (me, count))
    ]
    for copy in local:
        copy.wait()
    for r in range(rows):
        bound_ref[REACH + r : REACH + r + 1, :] = jnp.where(
            line < LANES // 2, low_ref[r], -high_ref[r]
        ).astype(jnp.float32)

    def own(field):
        ref = trace_ref if field < 2 else weight_ref
        return ref[field % 2].astype(jnp.float32)

    widths = (edge, REACH, REACH, REACH)
    starts = (0, edge, edge + REACH, edge + 2 * REACH)
    marks = roll(bound_ref[REACH : REACH + rows, :], (filled + LANES) // 2 - LANES // 2)
    for side in range(2):
        result = marks
        for field in reversed(range(4)):
            first = 0 if side else width - widths[field]
            result = jnp.where(
                line < starts[field] + widths[field],
                roll(own(field), starts[field] - first),
                result,
            )
        pack_ref[side] = result

    pl.semaphore_wait(barrier, beside[0] * beside[1] - 1)

    def part(di):
        return {-1: slice(0, REACH), 0: slice(0, rows), 1: slice(rows - REACH, rows)}[di]

    def halo_copies(di, dj):
        target = slot_of(-di, -dj)
        cut = part(di)
        if dj:
            pairs = ((pack_ref.at[(1 - dj) // 2], pack_recv.at[target]),)
        else:
            spot = (1 - di) // 2
            pairs = (
                (trace_ref.at[:, cut, :], trace_recv.at[spot, :, cut, :]),
                (weight_ref.at[:, cut, :], weight_recv.at[spot, :, cut, :]),
            )
        if dj and di:
            pairs = ((pack_ref.at[(1 - dj) // 2, cut, :], pack_recv.at[target, cut, :]),)
        return [
            pltpu.make_async_remote_copy(
                src_ref=source,
                dst_ref=landing,
                send_sem=send_sems.at[kind, slot_of(di, dj)],
                recv_sem=recv_sems.at[kind, target],
                device_id=device(di, dj),
                device_id_type=pl.DeviceIdType.MESH,
            )
            for kind, (source, landing) in enumerate(pairs)
        ]

    order = sorted(OFFSETS, key=lambda o: (o[0] == 0, o[1] == 0))
    for di, dj in order:

        @pl.when(present(di, dj))
        def _():
            for copy in halo_copies(di, dj):
                copy.start()

    for di, dj in OFFSETS:

        @pl.when(jnp.logical_not(present(di, dj)))
        def _():
            if dj:
                pack_recv[slot_of(di, dj)] = jnp.zeros((rows, width), jnp.float32)
            else:
                trace_recv[(1 + di) // 2] = jnp.zeros(trace_ref.shape, jnp.float32)
                weight_recv[(1 + di) // 2] = jnp.zeros(weight_ref.shape, jnp.int32)

    def arrive(di, dj):
        @pl.when(present(di, dj))
        def _():
            for copy in halo_copies(-di, -dj):
                copy.wait_recv()

    def windows(field, di):
        cut = part(-di)
        if di == 0:
            middle = own(field)
        else:
            landing = trace_recv if field < 2 else weight_recv
            middle = landing[(1 + di) // 2, field % 2, cut, :].astype(jnp.float32)
        left, right = (pack_recv[slot_of(di, dj), cut, :] for dj in (-1, 1))
        n = widths[field]
        turned = roll(middle, n)
        first = jnp.where(line < n, roll(left, -starts[field]), turned)
        rest = jnp.where(line < 2 * n, roll(right, n - starts[field]), 0.0)
        return first, jnp.where(line < n, turned, rest)

    def ahead_by(first, second, k):
        if k == 0:
            return first, second
        return roll(jnp.where(line < k, second, first), -k), roll(second, -k)

    tops = {-1: 0, 0: REACH, 1: REACH + rows}
    sizes = {-1: REACH, 0: rows, 1: REACH}

    def prepare(bank, parts, links):
        gap = LANES // SHIFTS // SUB * SUB
        far_at = dict(zip(parts, (0, -(-REACH // SUB) * SUB)))

        def place(ranges):
            spots, at = [], 0
            for start, stop in ranges:
                at += (start - at) % SUB
                spots.append((start, stop, at))
                at += stop - start
            assert at <= gap
            return spots

        cell_spots = place([(tops[di], tops[di] + sizes[di]) for di in parts])
        link_spots = place(links)
        for di, (_, _, at) in zip(parts, cell_spots):
            top, size = tops[di], sizes[di]
            pair = windows(0, di)
            for k in range(SHIFTS):
                for tile, x in enumerate(ahead_by(*pair, k)):
                    begin = k * gap + far_at[di]
                    plain_ref[bank, 1, tile, begin : begin + size, :] = x
            for tile, x in enumerate(windows(1, di)):
                plain_ref[bank, 0, tile, at : at + size, :] = x
            for tile, x in enumerate(windows(2, di)):
                inline_ref[tile, top : top + size, :] = x
            pair = windows(3, di)
            for tile, (x, y) in enumerate(zip(pair, ahead_by(*pair, 1))):
                plain_ref[bank, 0, tile, 2 * gap + at : 2 * gap + at + size, :] = (
                    FACE_SCALE * jnp.minimum(x, y)
                )
            if di:
                low = high_ = None
                for dj in (-1, 1):
                    marks = pack_recv[slot_of(di, dj), part(-di), :]
                    x, y = marks[:, filled : filled + 1], marks[:, LANES - 1 : LANES]
                    low = x if low is None else jnp.maximum(low, x)
                    high_ = y if high_ is None else jnp.minimum(high_, y)
                bound_ref[top : top + size, :] = jnp.where(line < LANES // 2, low, high_)
        for start, stop, at in link_spots:
            for tile in range(2):
                plain_ref[bank, 0, tile, gap + at : gap + at + stop - start, :] = (
                    FACE_SCALE
                    * jnp.minimum(
                        inline_ref[tile, start:stop, :], inline_ref[tile, start + 1 : stop + 1, :]
                    )
                )
        for kind in range(2):
            for tile in range(2):
                field_ref[bank, kind, tile * LANES : (tile + 1) * LANES, :] = jnp.transpose(
                    plain_ref[bank, kind, tile]
                )
        for c in range(chunk):
            piece = field_ref[bank, 0, pl.ds(c, PITCH, stride=chunk), :]
            block = jnp.transpose(jnp.concatenate([piece] * GROUPS, axis=0))
            for kind, spots in enumerate((cell_spots, link_spots, cell_spots)):
                for start, stop, at in spots:
                    face_ref[c, kind * high + start : kind * high + stop, :] = block[
                        kind * gap + at : kind * gap + at + stop - start
                    ]
        for y in range(0, chunk + SUB - 1, SHIFTS):
            pieces = [
                field_ref[bank, 1, pl.ds(y + g * SUB, PITCH, stride=chunk), :]
                for g in range(GROUPS)
            ]
            block = jnp.transpose(jnp.concatenate(pieces, axis=0))
            for k in range(SHIFTS):
                if y + k < deep:
                    for di in parts:
                        begin = k * gap + far_at[di]
                        far_ref[pl.ds(tops[di] * deep + y + k, sizes[di], stride=deep), :] = (
                            block[begin : begin + sizes[di]]
                        )

    sub = lax.broadcasted_iota(jnp.int32, (SUB, LANES), 0)
    lane = lax.broadcasted_iota(jnp.int32, (SUB, LANES), 1)
    lag = ((lane // PITCH) * SUB + sub).astype(jnp.float32)
    key = jnp.where(lane < LANES // 2, lag, -lag)

    def build(t, carry):
        penalty = jnp.where(key < bound_ref[pl.ds(t, 1), :], PENALTY, 0.0)
        for c in range(chunk):
            near = face_ref[c, pl.ds(t, 1), :]
            diff = near - far_ref[pl.ds(t * deep + c, SUB), :]
            m_ref[t, c] = diff * diff + penalty
        return carry

    for dj in (-1, 1):
        arrive(0, dj)
    prepare(0, (0,), [(REACH, REACH + rows - 1)])
    lax.fori_loop(REACH, REACH + rows, build, 0, unroll=4)

    for di, dj in OFFSETS:
        if di:
            arrive(di, dj)
    prepare(1, (-1, 1), [(0, REACH), (REACH + rows - 1, tall - 1)])
    lax.fori_loop(0, REACH, build, 0, unroll=5)
    lax.fori_loop(REACH + rows, tall, build, 0, unroll=5)

    for step in range(1, ITERS + 1):
        start, stop = step, tall - step

        def relax(t, state):
            here, before = state
            along = []
            for c in range(chunk):
                after = here[c + 1] if c < chunk - 1 else pltpu.roll(here[0], LANES - 1, 1)
                along.append(face_ref[c, pl.ds(2 * high + t, 1), :] * (after - here[c]))
            back = [pltpu.roll(along[-1], 1, 1)] + along[:-1]
            nexts, fluxes = [], []
            for c in range(chunk):
                ahead = m_ref[t + 1, c]
                across = face_ref[c, pl.ds(high + t, 1), :] * (ahead - here[c])
                m_ref[t, c] = (here[c] + (across - before[c])) + (along[c] - back[c])
                nexts.append(ahead)
                fluxes.append(across)
            return nexts, fluxes

        here = [m_ref[start, c] for c in range(chunk)]
        before = [
            face_ref[c, high + start - 1 : high + start, :] * (here[c] - m_ref[start - 1, c])
            for c in range(chunk)
        ]
        lax.fori_loop(start, stop, relax, (here, before), unroll=stop - start)

    for c in range(chunk):
        block = m_ref[REACH : REACH + rows, c].reshape(LANES, LANES)
        packed_ref[c * LANES : (c + 1) * LANES, :] = jnp.transpose(block)

    def unpack(x):
        return [roll(x, -v) for v in range(GROUPS)]

    spots = [lane % GROUPS == v for v in range(GROUPS)]

    def pack(xs):
        result = xs[0]
        for v in range(1, GROUPS):
            result = jnp.where(spots[v], roll(xs[v], v), result)
        return result

    def loose(index):
        return pl.ds(pl.multiple_of(index * SUB, SUB), SUB)

    @pl.when(me > 0)
    def _():
        def loosen(i, carry):
            for c in range(chunk):
                x = packed_ref[pl.ds(c * LANES + i, SUB, stride=PITCH), :]
                for v, y in enumerate(unpack(x)):
                    loose_ref[loose((i * chunk + c) * GROUPS + v), :] = y
            return carry

        lax.fori_loop(REACH // chunk, (width + REACH - 1) // chunk + 1, loosen, 0)

    last = width - 1
    state_copy = pltpu.make_async_remote_copy(
        src_ref=y_ref.at[last * SUB : (last + 1) * SUB, :],
        dst_ref=enter_ref,
        send_sem=send_sem,
        recv_sem=recv_sem,
        device_id={"tm": lax.min(me + 1, count - 1)},
        device_id_type=pl.DeviceIdType.MESH,
    )

    at_low = sub == 0
    at_high = sub == SUB - 1
    top = GROUPS - 1
    wide3 = [jnp.full((SUB, LANES), strain_ref[k]) >= 3 for k in range(width // STRETCH)]
    wide2 = [jnp.full((SUB, LANES), strain_ref[k]) >= 2 for k in range(width // STRETCH)]

    def below(x):
        return jnp.where(at_low, BIG, pltpu.roll(x, 1, 0))

    def above(x):
        return jnp.where(at_high, BIG, pltpu.roll(x, SUB - 1, 0))

    def advance(x, cost, k):
        x = [below(x[top])] + x + [above(x[0])]
        pair = [jnp.minimum(x[v], x[v + 1]) for v in range(GROUPS + 1)]
        one = [jnp.minimum(pair[v], pair[v + 1]) for v in range(GROUPS)]
        wide = [below(one[top - 1]), below(one[top])] + one + [above(one[0]), above(one[1])]
        two = [jnp.minimum(wide[v], wide[v + 2]) for v in range(GROUPS + 2)]
        three = [jnp.minimum(two[v], two[v + 2]) for v in range(GROUPS)]
        result = []
        for v in range(GROUPS):
            near = jnp.where(wide2[k], two[v + 1], one[v])
            result.append(cost[v] + jnp.where(wide3[k], three[v], near))
        return result

    @pl.when(me == 0)
    def _():
        state = [jnp.zeros((SUB, LANES), jnp.float32)] * GROUPS
        for s in range(width):
            x = s + REACH
            cost = unpack(packed_ref[pl.ds((x % chunk) * LANES + x // chunk, SUB, stride=PITCH), :])
            state = advance(state, cost, s // STRETCH)
            if s < last:
                for v in range(GROUPS):
                    loose_ref[loose(s * GROUPS + v), :] = state[v]
        y_ref[last * SUB : (last + 1) * SUB, :] = pack(state)

    @pl.when(me > 0)
    def _():
        state_copy.wait_recv()
        state = unpack(enter_ref[...])
        for s in range(width):
            cost = [loose_ref[loose((s + REACH) * GROUPS + v), :] for v in range(GROUPS)]
            state = advance(state, cost, s // STRETCH)
            y_ref[s * SUB : (s + 1) * SUB, :] = pack(state)

    @pl.when(me < count - 1)
    def _():
        state_copy.start()

    @pl.when(me == 0)
    def _():
        def tighten(s, carry):
            x = [loose_ref[loose(s * GROUPS + v), :] for v in range(GROUPS)]
            y_ref[pl.ds(pl.multiple_of(s * SUB, SUB), SUB), :] = pack(x)
            return carry

        lax.fori_loop(0, last, tighten, 0, unroll=4)

    @pl.when(me < count - 1)
    def _():
        state_copy.wait_send()

    for di, dj in OFFSETS:

        @pl.when(present(di, dj))
        def _():
            for copy in halo_copies(di, dj):
                copy.wait_send()


def spread(dims, y_ref, out_ref, turned_ref):
    rows, width = dims
    least = [None] * rows
    for g in range(SUB):
        block = jnp.transpose(y_ref[pl.ds(g, width, stride=SUB), :])
        turned_ref[g] = block
        for r in range(rows):
            tile = block[r * SUB : (r + 1) * SUB]
            least[r] = tile if g == 0 else jnp.minimum(least[r], tile)
    for r in range(rows):
        low = jnp.min(least[r], axis=0, keepdims=True)
        for g in range(SUB):
            tile = turned_ref[g, r * SUB : (r + 1) * SUB, :] - low
            out_ref[pl.ds(g * SUB * rows + r, SUB, stride=rows), :] = tile


def per_device(near_trace, far_trace, inline_weight, time_weight, lag_low, lag_high, strain):
    rows, width = near_trace.shape
    count = lax.axis_size("tm")
    count_in = lax.axis_size("inline")
    tall = rows + 2 * REACH
    high = -(-tall // SUB) * SUB
    chunk = -(-(width + 2 * REACH) // PITCH)
    deep = -(-(chunk + SUB - 1) // SUB) * SUB
    assert width == LANES and rows * SUB == LANES and SHIFTS * high <= LANES
    assert REACH + HALF + 3 * REACH < LANES - SUB and REACH <= rows
    assert chunk * PITCH + L <= 2 * LANES and REACH + HALF <= width
    vmem = pl.BlockSpec(memory_space=pltpu.VMEM)
    packed = pl.pallas_call(
        functools.partial(kernel, (rows, width, count, count_in, tall, high, chunk, deep)),
        out_shape=jax.ShapeDtypeStruct((width * SUB, LANES), jnp.float32),
        in_specs=[pl.BlockSpec(memory_space=pltpu.HBM)] * 7,
        out_specs=vmem,
        scratch_shapes=[
            pltpu.VMEM((2, rows, width), jnp.float32),
            pltpu.VMEM((2, rows, width), jnp.int32),
            pltpu.VMEM((2, rows, width), jnp.float32),
            pltpu.VMEM((2, 2, rows, width), jnp.float32),
            pltpu.VMEM((2, 2, rows, width), jnp.int32),
            pltpu.VMEM((9, rows, width), jnp.float32),
            pltpu.VMEM((2, 2, 2, LANES, LANES), jnp.float32),
            pltpu.VMEM((2, high, LANES), jnp.float32),
            pltpu.VMEM((2, 2, 2 * LANES, LANES), jnp.float32),
            pltpu.VMEM((chunk, LANES, LANES), jnp.float32),
            pltpu.VMEM((tall * deep, LANES), jnp.float32),
            pltpu.VMEM((high, LANES), jnp.float32),
            pltpu.VMEM((tall, chunk, SUB, LANES), jnp.float32),
            pltpu.VMEM((chunk * LANES, LANES), jnp.float32),
            pltpu.VMEM((chunk * PITCH * GROUPS * SUB, LANES), jnp.float32),
            pltpu.VMEM((SUB, LANES), jnp.float32),
            pltpu.SMEM(lag_low.shape, jnp.int32),
            pltpu.SMEM(lag_high.shape, jnp.int32),
            pltpu.SMEM(strain.shape, jnp.int32),
            pltpu.SemaphoreType.DMA((7,)),
            pltpu.SemaphoreType.DMA((2, 9)),
            pltpu.SemaphoreType.DMA((2, 9)),
            pltpu.SemaphoreType.DMA,
            pltpu.SemaphoreType.DMA,
        ],
        compiler_params=pltpu.CompilerParams(
            collective_id=0, has_side_effects=True, vmem_limit_bytes=24 << 20
        ),
    )(
        *[
            pltpu.with_memory_space_constraint(x, pltpu.HBM)
            for x in (far_trace, near_trace, inline_weight, time_weight, lag_low, lag_high, strain)
        ]
    )
    out = pl.pallas_call(
        functools.partial(spread, (rows, width)),
        out_shape=jax.ShapeDtypeStruct((L * rows, width), jnp.float32),
        in_specs=[vmem],
        out_specs=vmem,
        scratch_shapes=[pltpu.VMEM((SUB, LANES, width), jnp.float32)],
        compiler_params=pltpu.CompilerParams(vmem_limit_bytes=24 << 20),
    )(packed)
    return out.reshape(L, rows, width)


def solution(mesh):
    return jax.shard_map(
        per_device,
        mesh=mesh,
        in_specs=(
            P(("group", "inline"), "tm"),
            P(("group", "inline"), "tm"),
            P(("group", "inline"), "tm"),
            P(("group", "inline"), "tm"),
            P(("group", "inline")),
            P(("group", "inline")),
            P(("group", "tm")),
        ),
        out_specs=P(None, ("group", "inline"), "tm"),
        check_vma=False,
    )
```

```python
import functools

import jax
import jax.numpy as jnp
from jax import lax
from jax.experimental import pallas as pl
from jax.experimental.pallas import tpu as pltpu
from jax.sharding import PartitionSpec as P

L = 64
STRETCH = 64
ITERS = 10

BIG = 1000000000.0
PENALTY = 2.0
FACE_SCALE = 0.016

SUB = 8
LANES = 128
GROUPS = L // SUB
HALF = L // 2
REACH = ITERS
PITCH = LANES // GROUPS
SHIFTS = 3

OFFSETS = [(di, dj) for di in (-1, 0, 1) for dj in (-1, 0, 1) if (di, dj) != (0, 0)]


def slot_of(di, dj):
    return (di + 1) * 3 + dj + 1


def roll(x, shift, axis=1):
    shift %= x.shape[axis]
    return pltpu.roll(x, shift, axis) if shift else x


def kernel(
    dims,
    far_in,
    near_in,
    inline_in,
    time_in,
    low_in,
    high_in,
    strain_in,
    y_ref,
    trace_ref,
    weight_ref,
    pack_ref,
    trace_recv,
    weight_recv,
    pack_recv,
    plain_ref,
    inline_ref,
    field_ref,
    face_ref,
    far_ref,
    bound_ref,
    m_ref,
    link_ref,
    packed_ref,
    loose_ref,
    enter_ref,
    leave_ref,
    low_ref,
    high_ref,
    strain_ref,
    local_sems,
    send_sems,
    recv_sems,
    send_sem,
    recv_sem,
):
    rows, width, count, count_in, tall, high, chunk, deep = dims
    edge = REACH + HALF
    filled = edge + 3 * REACH
    me = lax.axis_index("tm")
    here_in = lax.axis_index("inline")

    def present(di, dj):
        ok = None
        for step, place, total in ((di, here_in, count_in), (dj, me, count)):
            if step:
                inside = (place + step >= 0) & (place + step < total)
                ok = inside if ok is None else ok & inside
        return ok

    def device(di, dj):
        return {
            "inline": lax.clamp(0, here_in + di, count_in - 1),
            "tm": lax.clamp(0, me + dj, count - 1),
        }

    local = [
        pltpu.make_async_copy(source, target, local_sems.at[k])
        for k, (source, target) in enumerate(
            (
                (far_in, trace_ref.at[0]),
                (near_in, trace_ref.at[1]),
                (inline_in, weight_ref.at[0]),
                (time_in, weight_ref.at[1]),
                (low_in, low_ref),
                (high_in, high_ref),
                (strain_in, strain_ref),
            )
        )
    ]
    for copy in local:
        copy.start()

    line = lax.broadcasted_iota(jnp.int32, (1, LANES), 1)
    barrier = pltpu.get_barrier_semaphore()
    for di, dj in OFFSETS:

        @pl.when(present(di, dj))
        def _():
            pl.semaphore_signal(
                barrier, inc=1, device_id=device(di, dj), device_id_type=pl.DeviceIdType.MESH
            )

    beside = [
        1 + (place > 0).astype(jnp.int32) + (place < total - 1).astype(jnp.int32)
        for place, total in ((here_in, count_in), (me, count))
    ]
    for copy in local:
        copy.wait()
    for r in range(rows):
        bound_ref[REACH + r : REACH + r + 1, :] = jnp.where(
            line < LANES // 2, low_ref[r], -high_ref[r]
        ).astype(jnp.float32)

    def own(field):
        ref = trace_ref if field < 2 else weight_ref
        return ref[field % 2].astype(jnp.float32)

    widths = (edge, REACH, REACH, REACH)
    starts = (0, edge, edge + REACH, edge + 2 * REACH)
    marks = roll(bound_ref[REACH : REACH + rows, :], (filled + LANES) // 2 - LANES // 2)
    for side in range(2):
        result = marks
        for field in reversed(range(4)):
            first = 0 if side else width - widths[field]
            result = jnp.where(
                line < starts[field] + widths[field],
                roll(own(field), starts[field] - first),
                result,
            )
        pack_ref[side] = result

    pl.semaphore_wait(barrier, beside[0] * beside[1] - 1)

    def part(di):
        return {-1: slice(0, REACH), 0: slice(0, rows), 1: slice(rows - REACH, rows)}[di]

    def halo_copies(di, dj):
        target = slot_of(-di, -dj)
        cut = part(di)
        if dj:
            pairs = ((pack_ref.at[(1 - dj) // 2], pack_recv.at[target]),)
        else:
            spot = (1 - di) // 2
            pairs = (
                (trace_ref.at[:, cut, :], trace_recv.at[spot, :, cut, :]),
                (weight_ref.at[:, cut, :], weight_recv.at[spot, :, cut, :]),
            )
        if dj and di:
            pairs = ((pack_ref.at[(1 - dj) // 2, cut, :], pack_recv.at[target, cut, :]),)
        return [
            pltpu.make_async_remote_copy(
                src_ref=source,
                dst_ref=landing,
                send_sem=send_sems.at[kind, slot_of(di, dj)],
                recv_sem=recv_sems.at[kind, target],
                device_id=device(di, dj),
                device_id_type=pl.DeviceIdType.MESH,
            )
            for kind, (source, landing) in enumerate(pairs)
        ]

    order = sorted(OFFSETS, key=lambda o: (o[0] == 0, o[1] == 0))
    for di, dj in order:

        @pl.when(present(di, dj))
        def _():
            for copy in halo_copies(di, dj):
                copy.start()

    for di, dj in OFFSETS:

        @pl.when(jnp.logical_not(present(di, dj)))
        def _():
            if dj:
                pack_recv[slot_of(di, dj)] = jnp.zeros((rows, width), jnp.float32)
            else:
                trace_recv[(1 + di) // 2] = jnp.zeros(trace_ref.shape, jnp.float32)
                weight_recv[(1 + di) // 2] = jnp.zeros(weight_ref.shape, jnp.int32)

    def arrive(di, dj):
        @pl.when(present(di, dj))
        def _():
            for copy in halo_copies(-di, -dj):
                copy.wait_recv()

    def windows(field, di):
        cut = part(-di)
        if di == 0:
            middle = own(field)
        else:
            landing = trace_recv if field < 2 else weight_recv
            middle = landing[(1 + di) // 2, field % 2, cut, :].astype(jnp.float32)
        left, right = (pack_recv[slot_of(di, dj), cut, :] for dj in (-1, 1))
        n = widths[field]
        turned = roll(middle, n)
        first = jnp.where(line < n, roll(left, -starts[field]), turned)
        rest = jnp.where(line < 2 * n, roll(right, n - starts[field]), 0.0)
        return first, jnp.where(line < n, turned, rest)

    def ahead_by(first, second, k):
        if k == 0:
            return first, second
        return roll(jnp.where(line < k, second, first), -k), roll(second, -k)

    tops = {-1: 0, 0: REACH, 1: REACH + rows}
    sizes = {-1: REACH, 0: rows, 1: REACH}

    def prepare(bank, parts, links):
        gap = LANES // SHIFTS // SUB * SUB
        far_at = dict(zip(parts, (0, -(-REACH // SUB) * SUB)))

        def place(ranges):
            spots, at = [], 0
            for start, stop in ranges:
                at += (start - at) % SUB
                spots.append((start, stop, at))
                at += stop - start
            assert at <= gap
            return spots

        cell_spots = place([(tops[di], tops[di] + sizes[di]) for di in parts])
        link_spots = place(links)
        for di, (_, _, at) in zip(parts, cell_spots):
            top, size = tops[di], sizes[di]
            pair = windows(0, di)
            for k in range(SHIFTS):
                for tile, x in enumerate(ahead_by(*pair, k)):
                    begin = k * gap + far_at[di]
                    plain_ref[bank, 1, tile, begin : begin + size, :] = x
            for tile, x in enumerate(windows(1, di)):
                plain_ref[bank, 0, tile, at : at + size, :] = x
            for tile, x in enumerate(windows(2, di)):
                inline_ref[tile, top : top + size, :] = x
            pair = windows(3, di)
            for tile, (x, y) in enumerate(zip(pair, ahead_by(*pair, 1))):
                plain_ref[bank, 0, tile, 2 * gap + at : 2 * gap + at + size, :] = (
                    FACE_SCALE * jnp.minimum(x, y)
                )
            if di:
                low = high_ = None
                for dj in (-1, 1):
                    marks = pack_recv[slot_of(di, dj), part(-di), :]
                    x, y = marks[:, filled : filled + 1], marks[:, LANES - 1 : LANES]
                    low = x if low is None else jnp.maximum(low, x)
                    high_ = y if high_ is None else jnp.minimum(high_, y)
                bound_ref[top : top + size, :] = jnp.where(line < LANES // 2, low, high_)
        for start, stop, at in link_spots:
            for tile in range(2):
                plain_ref[bank, 0, tile, gap + at : gap + at + stop - start, :] = (
                    FACE_SCALE
                    * jnp.minimum(
                        inline_ref[tile, start:stop, :], inline_ref[tile, start + 1 : stop + 1, :]
                    )
                )
        for kind in range(2):
            for tile in range(2):
                field_ref[bank, kind, tile * LANES : (tile + 1) * LANES, :] = jnp.transpose(
                    plain_ref[bank, kind, tile]
                )
        for c in range(chunk):
            piece = field_ref[bank, 0, pl.ds(c, PITCH, stride=chunk), :]
            block = jnp.transpose(jnp.concatenate([piece] * GROUPS, axis=0))
            for kind, spots in enumerate((cell_spots, link_spots, cell_spots)):
                for start, stop, at in spots:
                    face_ref[c, kind * high + start : kind * high + stop, :] = block[
                        kind * gap + at : kind * gap + at + stop - start
                    ]
        for y in range(0, chunk + SUB - 1, SHIFTS):
            pieces = [
                field_ref[bank, 1, pl.ds(y + g * SUB, PITCH, stride=chunk), :]
                for g in range(GROUPS)
            ]
            block = jnp.transpose(jnp.concatenate(pieces, axis=0))
            for k in range(SHIFTS):
                if y + k < deep:
                    for di in parts:
                        begin = k * gap + far_at[di]
                        far_ref[pl.ds(tops[di] * deep + y + k, sizes[di], stride=deep), :] = (
                            block[begin : begin + sizes[di]]
                        )

    sub = lax.broadcasted_iota(jnp.int32, (SUB, LANES), 0)
    lane = lax.broadcasted_iota(jnp.int32, (SUB, LANES), 1)
    lag = ((lane // PITCH) * SUB + sub).astype(jnp.float32)
    key = jnp.where(lane < LANES // 2, lag, -lag)

    def build(t, carry):
        penalty = jnp.where(key < bound_ref[pl.ds(t, 1), :], PENALTY, 0.0)
        for c in range(chunk):
            near = face_ref[c, pl.ds(t, 1), :]
            diff = near - far_ref[pl.ds(t * deep + c, SUB), :]
            m_ref[t, c] = diff * diff + penalty
        return carry

    def weight(kind, c, t):
        return face_ref[c, pl.ds(kind * high + t, 1), :]

    def update(t, here, before, across):
        along = []
        for c in range(chunk):
            after = here[c + 1] if c < chunk - 1 else pltpu.roll(here[0], LANES - 1, 1)
            along.append(weight(2, c, t) * (after - here[c]))
        back = [pltpu.roll(along[-1], 1, 1)] + along[:-1]
        for c in range(chunk):
            m_ref[t, c] = (here[c] + (across[c] - before[c])) + (along[c] - back[c])

    def link(t, here, ahead):
        return [weight(1, c, t) * (ahead[c] - here[c]) for c in range(chunk)]

    def row(t):
        return [m_ref[t, c] for c in range(chunk)]

    def relax(t, state):
        here, before = state
        ahead = row(t + 1)
        across = link(t, here, ahead)
        update(t, here, before, across)
        return ahead, across

    def sweep(start, stop, before=None):
        here = row(start)
        if before is None:
            before = link(start - 1, row(start - 1), here)
        return lax.fori_loop(start, stop, relax, (here, before), unroll=stop - start)

    for dj in (-1, 1):
        arrive(0, dj)
    prepare(0, (0,), [(REACH, REACH + rows - 1)])
    lax.fori_loop(REACH, REACH + rows, build, 0, unroll=4)

    inner = min(2, (rows - 1) // 2)
    for step in range(1, min(inner, ITERS) + 1):
        start, stop = REACH + step, REACH + rows - step
        first = link(start - 1, row(start - 1), row(start))
        _, last_link = sweep(start, stop, first)
        for c in range(chunk):
            link_ref[0, step - 1, c] = first[c]
            link_ref[1, step - 1, c] = last_link[c]

    for di, dj in OFFSETS:
        if di:
            arrive(di, dj)
    prepare(1, (-1, 1), [(0, REACH), (REACH + rows - 1, tall - 1)])
    lax.fori_loop(0, REACH, build, 0, unroll=5)
    lax.fori_loop(REACH + rows, tall, build, 0, unroll=5)

    for step in range(1, ITERS):
        if step > inner:
            sweep(step, tall - step)
            continue
        edge_row = REACH + step - 1
        here, before = sweep(step, edge_row)
        update(edge_row, here, before, [link_ref[0, step - 1, c] for c in range(chunk)])
        first = [link_ref[1, step - 1, c] for c in range(chunk)]
        sweep(REACH + rows - step, tall - step, first)

    kept = range(REACH, REACH + rows)
    back = {}
    for t in kept:
        along = weight(2, chunk - 1, t) * (
            pltpu.roll(m_ref[t, 0], LANES - 1, 1) - m_ref[t, chunk - 1]
        )
        back[t] = (pltpu.roll(along, 1, 1), along)
    for c in range(chunk):
        here = m_ref[REACH, c]
        before = weight(1, c, REACH - 1) * (here - m_ref[REACH - 1, c])
        fresh = []
        for t in kept:
            ahead = m_ref[t + 1, c]
            across = weight(1, c, t) * (ahead - here)
            if c < chunk - 1:
                along = weight(2, c, t) * (m_ref[t, c + 1] - here)
            else:
                along = back[t][1]
            fresh.append((here + (across - before)) + (along - back[t][0]))
            back[t] = (along, back[t][1])
            here, before = ahead, across
        packed_ref[c * LANES : (c + 1) * LANES, :] = jnp.transpose(
            jnp.concatenate(fresh, axis=0)
        )

    def unpack(x):
        return [roll(x, -v) for v in range(GROUPS)]

    spots = [lane % GROUPS == v for v in range(GROUPS)]

    def pack(xs):
        result = xs[0]
        for v in range(1, GROUPS):
            result = jnp.where(spots[v], roll(xs[v], v), result)
        return result

    def loose(index):
        return pl.ds(pl.multiple_of(index * SUB, SUB), SUB)

    @pl.when(me > 0)
    def _():
        def loosen(i, carry):
            for c in range(chunk):
                x = packed_ref[pl.ds(c * LANES + i, SUB, stride=PITCH), :]
                for v, y in enumerate(unpack(x)):
                    loose_ref[loose((i * chunk + c) * GROUPS + v), :] = y
            return carry

        lax.fori_loop(REACH // chunk, (width + REACH - 1) // chunk + 1, loosen, 0)

    state_copy = pltpu.make_async_remote_copy(
        src_ref=leave_ref,
        dst_ref=enter_ref,
        send_sem=send_sem,
        recv_sem=recv_sem,
        device_id={"tm": lax.min(me + 1, count - 1)},
        device_id_type=pl.DeviceIdType.MESH,
    )

    at_low = sub == 0
    at_high = sub == SUB - 1
    top = GROUPS - 1
    wide3 = [jnp.full((SUB, LANES), strain_ref[k]) >= 3 for k in range(width // STRETCH)]
    wide2 = [jnp.full((SUB, LANES), strain_ref[k]) >= 2 for k in range(width // STRETCH)]

    def below(x):
        return jnp.where(at_low, BIG, pltpu.roll(x, 1, 0))

    def above(x):
        return jnp.where(at_high, BIG, pltpu.roll(x, SUB - 1, 0))

    def advance(x, cost, k):
        x = [below(x[top])] + x + [above(x[0])]
        pair = [jnp.minimum(x[v], x[v + 1]) for v in range(GROUPS + 1)]
        one = [jnp.minimum(pair[v], pair[v + 1]) for v in range(GROUPS)]
        wide = [below(one[top - 1]), below(one[top])] + one + [above(one[0]), above(one[1])]
        two = [jnp.minimum(wide[v], wide[v + 2]) for v in range(GROUPS + 2)]
        three = [jnp.minimum(two[v], two[v + 2]) for v in range(GROUPS)]
        result = []
        for v in range(GROUPS):
            near = jnp.where(wide2[k], two[v + 1], one[v])
            result.append(cost[v] + jnp.where(wide3[k], three[v], near))
        return result

    @pl.when(me == 0)
    def _():
        state = [jnp.zeros((SUB, LANES), jnp.float32)] * GROUPS
        for s in range(width):
            x = s + REACH
            cost = unpack(packed_ref[pl.ds((x % chunk) * LANES + x // chunk, SUB, stride=PITCH), :])
            state = advance(state, cost, s // STRETCH)
            for v in range(GROUPS):
                loose_ref[loose(s * GROUPS + v), :] = state[v]
        leave_ref[...] = pack(state)

    def follow(final):
        state_copy.wait_recv()
        state = unpack(enter_ref[...])
        for s in range(width):
            spots_s = [loose((s + REACH) * GROUPS + v) for v in range(GROUPS)]
            state = advance(state, [loose_ref[spot, :] for spot in spots_s], s // STRETCH)
            if final:
                y_ref[s * SUB : (s + 1) * SUB, :] = pack(state)
            else:
                for v in range(GROUPS):
                    loose_ref[loose(s * GROUPS + v), :] = state[v]
        if not final:
            leave_ref[...] = pack(state)

    @pl.when((me > 0) & (me < count - 1))
    def _():
        follow(False)

    @pl.when((me > 0) & (me == count - 1))
    def _():
        follow(True)

    @pl.when(me < count - 1)
    def _():
        state_copy.start()

    @pl.when(me < count - 1)
    def _():
        def tighten(s, carry):
            x = [loose_ref[loose(s * GROUPS + v), :] for v in range(GROUPS)]
            y_ref[pl.ds(pl.multiple_of(s * SUB, SUB), SUB), :] = pack(x)
            return carry

        lax.fori_loop(0, width, tighten, 0, unroll=16)

    @pl.when(me < count - 1)
    def _():
        state_copy.wait_send()

    for di, dj in OFFSETS:

        @pl.when(present(di, dj))
        def _():
            for copy in halo_copies(di, dj):
                copy.wait_send()


def spread(dims, y_ref, out_ref, ready_ref, sems):
    rows, width = dims
    blocks = [y_ref[pl.ds(g, width, stride=SUB), :] for g in range(SUB)]
    low = jnp.transpose(functools.reduce(jnp.minimum, blocks))
    least = [
        jnp.min(low[r * SUB : (r + 1) * SUB], axis=0, keepdims=True) for r in range(rows)
    ]
    copies = []
    for g in range(SUB):
        block = jnp.transpose(blocks[g])
        for r in range(rows):
            ready_ref[pl.ds(g * SUB * rows + r, SUB, stride=rows), :] = (
                block[r * SUB : (r + 1) * SUB] - least[r]
            )
        piece = pl.ds(g * SUB * rows, SUB * rows)
        copies.append(
            pltpu.make_async_copy(ready_ref.at[piece, :], out_ref.at[piece, :], sems.at[g])
        )
        copies[-1].start()
    for copy in copies:
        copy.wait()


def per_device(near_trace, far_trace, inline_weight, time_weight, lag_low, lag_high, strain):
    rows, width = near_trace.shape
    count = lax.axis_size("tm")
    count_in = lax.axis_size("inline")
    tall = rows + 2 * REACH
    high = -(-tall // SUB) * SUB
    chunk = -(-(width + 2 * REACH) // PITCH)
    deep = -(-(chunk + SUB - 1) // SUB) * SUB
    assert width == LANES and rows * SUB == LANES and SHIFTS * high <= LANES
    assert REACH + HALF + 3 * REACH < LANES - SUB and REACH <= rows
    assert chunk * PITCH + L <= 2 * LANES and REACH + HALF <= width
    vmem = pl.BlockSpec(memory_space=pltpu.VMEM)
    packed = pl.pallas_call(
        functools.partial(kernel, (rows, width, count, count_in, tall, high, chunk, deep)),
        out_shape=jax.ShapeDtypeStruct((width * SUB, LANES), jnp.float32),
        in_specs=[pl.BlockSpec(memory_space=pltpu.HBM)] * 7,
        out_specs=vmem,
        scratch_shapes=[
            pltpu.VMEM((2, rows, width), jnp.float32),
            pltpu.VMEM((2, rows, width), jnp.int32),
            pltpu.VMEM((2, rows, width), jnp.float32),
            pltpu.VMEM((2, 2, rows, width), jnp.float32),
            pltpu.VMEM((2, 2, rows, width), jnp.int32),
            pltpu.VMEM((9, rows, width), jnp.float32),
            pltpu.VMEM((2, 2, 2, LANES, LANES), jnp.float32),
            pltpu.VMEM((2, high, LANES), jnp.float32),
            pltpu.VMEM((2, 2, 2 * LANES, LANES), jnp.float32),
            pltpu.VMEM((chunk, LANES, LANES), jnp.float32),
            pltpu.VMEM((tall * deep, LANES), jnp.float32),
            pltpu.VMEM((high, LANES), jnp.float32),
            pltpu.VMEM((tall, chunk, SUB, LANES), jnp.float32),
            pltpu.VMEM((2, (rows - 1) // 2, chunk, SUB, LANES), jnp.float32),
            pltpu.VMEM((chunk * LANES, LANES), jnp.float32),
            pltpu.VMEM((chunk * PITCH * GROUPS * SUB, LANES), jnp.float32),
            pltpu.VMEM((SUB, LANES), jnp.float32),
            pltpu.VMEM((SUB, LANES), jnp.float32),
            pltpu.SMEM(lag_low.shape, jnp.int32),
            pltpu.SMEM(lag_high.shape, jnp.int32),
            pltpu.SMEM(strain.shape, jnp.int32),
            pltpu.SemaphoreType.DMA((7,)),
            pltpu.SemaphoreType.DMA((2, 9)),
            pltpu.SemaphoreType.DMA((2, 9)),
            pltpu.SemaphoreType.DMA,
            pltpu.SemaphoreType.DMA,
        ],
        compiler_params=pltpu.CompilerParams(
            collective_id=0, has_side_effects=True, vmem_limit_bytes=24 << 20
        ),
    )(
        *[
            pltpu.with_memory_space_constraint(x, pltpu.HBM)
            for x in (far_trace, near_trace, inline_weight, time_weight, lag_low, lag_high, strain)
        ]
    )
    out = pl.pallas_call(
        functools.partial(spread, (rows, width)),
        out_shape=jax.ShapeDtypeStruct((L * rows, width), jnp.float32),
        in_specs=[vmem],
        out_specs=pl.BlockSpec(memory_space=pltpu.HBM),
        scratch_shapes=[
            pltpu.VMEM((L * rows, width), jnp.float32),
            pltpu.SemaphoreType.DMA((SUB,)),
        ],
        compiler_params=pltpu.CompilerParams(vmem_limit_bytes=24 << 20),
    )(packed)
    return out.reshape(L, rows, width)


def solution(mesh):
    return jax.shard_map(
        per_device,
        mesh=mesh,
        in_specs=(
            P(("group", "inline"), "tm"),
            P(("group", "inline"), "tm"),
            P(("group", "inline"), "tm"),
            P(("group", "inline"), "tm"),
            P(("group", "inline")),
            P(("group", "inline")),
            P(("group", "tm")),
        ),
        out_specs=P(None, ("group", "inline"), "tm"),
        check_vma=False,
    )
```

```python
import functools

import jax
import jax.numpy as jnp
from jax import lax
from jax.experimental import pallas as pl
from jax.experimental.pallas import tpu as pltpu
from jax.sharding import PartitionSpec as P

L = 64
STRETCH = 64
ITERS = 10

BIG = 1000000000.0
PENALTY = 2.0
FACE_SCALE = 0.016

SUB = 8
LANES = 128
GROUPS = L // SUB
HALF = L // 2
REACH = ITERS
PITCH = LANES // GROUPS
SHIFTS = 3

OFFSETS = [(di, dj) for di in (-1, 0, 1) for dj in (-1, 0, 1) if (di, dj) != (0, 0)]


def slot_of(di, dj):
    return (di + 1) * 3 + dj + 1


def roll(x, shift, axis=1):
    shift %= x.shape[axis]
    return pltpu.roll(x, shift, axis) if shift else x


def kernel(
    dims,
    far_in,
    near_in,
    inline_in,
    time_in,
    low_in,
    high_in,
    strain_in,
    y_ref,
    trace_ref,
    weight_ref,
    pack_ref,
    trace_recv,
    weight_recv,
    pack_recv,
    plain_ref,
    inline_ref,
    field_ref,
    face_ref,
    far_ref,
    bound_ref,
    m_ref,
    link_ref,
    packed_ref,
    loose_ref,
    enter_ref,
    leave_ref,
    low_ref,
    high_ref,
    strain_ref,
    local_sems,
    send_sems,
    recv_sems,
    send_sem,
    recv_sem,
):
    rows, width, count, count_in, tall, high, chunk, deep = dims
    edge = REACH + HALF
    filled = edge + 3 * REACH
    me = lax.axis_index("tm")
    here_in = lax.axis_index("inline")

    def present(di, dj):
        ok = None
        for step, place, total in ((di, here_in, count_in), (dj, me, count)):
            if step:
                inside = (place + step >= 0) & (place + step < total)
                ok = inside if ok is None else ok & inside
        return ok

    def device(di, dj):
        return {
            "inline": lax.clamp(0, here_in + di, count_in - 1),
            "tm": lax.clamp(0, me + dj, count - 1),
        }

    local = [
        pltpu.make_async_copy(source, target, local_sems.at[k])
        for k, (source, target) in enumerate(
            (
                (far_in, trace_ref.at[0]),
                (near_in, trace_ref.at[1]),
                (inline_in, weight_ref.at[0]),
                (time_in, weight_ref.at[1]),
                (low_in, low_ref),
                (high_in, high_ref),
                (strain_in, strain_ref),
            )
        )
    ]
    for copy in local:
        copy.start()

    line = lax.broadcasted_iota(jnp.int32, (1, LANES), 1)
    barrier = pltpu.get_barrier_semaphore()
    for di, dj in OFFSETS:

        @pl.when(present(di, dj))
        def _():
            pl.semaphore_signal(
                barrier, inc=1, device_id=device(di, dj), device_id_type=pl.DeviceIdType.MESH
            )

    beside = [
        1 + (place > 0).astype(jnp.int32) + (place < total - 1).astype(jnp.int32)
        for place, total in ((here_in, count_in), (me, count))
    ]
    for copy in local:
        copy.wait()
    for r in range(rows):
        bound_ref[REACH + r : REACH + r + 1, :] = jnp.where(
            line < LANES // 2, low_ref[r], -high_ref[r]
        ).astype(jnp.float32)

    def own(field):
        ref = trace_ref if field < 2 else weight_ref
        return ref[field % 2].astype(jnp.float32)

    widths = (edge, REACH, REACH, REACH)
    starts = (0, edge, edge + REACH, edge + 2 * REACH)
    marks = roll(bound_ref[REACH : REACH + rows, :], (filled + LANES) // 2 - LANES // 2)
    for side in range(2):
        result = marks
        for field in reversed(range(4)):
            first = 0 if side else width - widths[field]
            result = jnp.where(
                line < starts[field] + widths[field],
                roll(own(field), starts[field] - first),
                result,
            )
        pack_ref[side] = result

    pl.semaphore_wait(barrier, beside[0] * beside[1] - 1)

    def part(di):
        return {-1: slice(0, REACH), 0: slice(0, rows), 1: slice(rows - REACH, rows)}[di]

    def halo_copies(di, dj):
        target = slot_of(-di, -dj)
        cut = part(di)
        if dj:
            pairs = ((pack_ref.at[(1 - dj) // 2], pack_recv.at[target]),)
        else:
            spot = (1 - di) // 2
            pairs = (
                (trace_ref.at[:, cut, :], trace_recv.at[spot, :, cut, :]),
                (weight_ref.at[:, cut, :], weight_recv.at[spot, :, cut, :]),
            )
        if dj and di:
            pairs = ((pack_ref.at[(1 - dj) // 2, cut, :], pack_recv.at[target, cut, :]),)
        return [
            pltpu.make_async_remote_copy(
                src_ref=source,
                dst_ref=landing,
                send_sem=send_sems.at[kind, slot_of(di, dj)],
                recv_sem=recv_sems.at[kind, target],
                device_id=device(di, dj),
                device_id_type=pl.DeviceIdType.MESH,
            )
            for kind, (source, landing) in enumerate(pairs)
        ]

    order = sorted(OFFSETS, key=lambda o: (o[0] == 0, o[1] == 0))
    for di, dj in order:

        @pl.when(present(di, dj))
        def _():
            for copy in halo_copies(di, dj):
                copy.start()

    for di, dj in OFFSETS:

        @pl.when(jnp.logical_not(present(di, dj)))
        def _():
            if dj:
                pack_recv[slot_of(di, dj)] = jnp.zeros((rows, width), jnp.float32)
            else:
                trace_recv[(1 + di) // 2] = jnp.zeros(trace_ref.shape, jnp.float32)
                weight_recv[(1 + di) // 2] = jnp.zeros(weight_ref.shape, jnp.int32)

    def arrive(di, dj):
        @pl.when(present(di, dj))
        def _():
            for copy in halo_copies(-di, -dj):
                copy.wait_recv()

    def windows(field, di):
        cut = part(-di)
        if di == 0:
            middle = own(field)
        else:
            landing = trace_recv if field < 2 else weight_recv
            middle = landing[(1 + di) // 2, field % 2, cut, :].astype(jnp.float32)
        left, right = (pack_recv[slot_of(di, dj), cut, :] for dj in (-1, 1))
        n = widths[field]
        turned = roll(middle, n)
        first = jnp.where(line < n, roll(left, -starts[field]), turned)
        rest = jnp.where(line < 2 * n, roll(right, n - starts[field]), 0.0)
        return first, jnp.where(line < n, turned, rest)

    def ahead_by(first, second, k):
        if k == 0:
            return first, second
        return roll(jnp.where(line < k, second, first), -k), roll(second, -k)

    tops = {-1: 0, 0: REACH, 1: REACH + rows}
    sizes = {-1: REACH, 0: rows, 1: REACH}

    def prepare(bank, parts, links):
        def place(ranges):
            spots, at = [], 0
            for start, stop in ranges:
                spots.append((start, stop, at))
                at += stop - start
            return spots, at

        cell_spots, unit = place([(tops[di], tops[di] + sizes[di]) for di in parts])
        link_spots, used = place(links)
        assert used <= unit and 6 * unit <= LANES
        shifts = LANES // unit
        for di, (top, stop, at) in zip(parts, cell_spots):
            size = stop - top
            pair = windows(0, di)
            for k in range(shifts):
                for tile, x in enumerate(ahead_by(*pair, k)):
                    begin = k * unit + at
                    plain_ref[bank, 1, tile, begin : begin + size, :] = x
            for tile, x in enumerate(windows(1, di)):
                plain_ref[bank, 0, tile, at : at + size, :] = x
            for tile, x in enumerate(windows(2, di)):
                inline_ref[tile, top:stop, :] = x
            pair = windows(3, di)
            for tile, (x, y) in enumerate(zip(pair, ahead_by(*pair, 1))):
                plain_ref[bank, 0, tile, 2 * unit + at : 2 * unit + at + size, :] = (
                    FACE_SCALE * jnp.minimum(x, y)
                )
            if di:
                low = high_ = None
                for dj in (-1, 1):
                    marks = pack_recv[slot_of(di, dj), part(-di), :]
                    x, y = marks[:, filled : filled + 1], marks[:, LANES - 1 : LANES]
                    low = x if low is None else jnp.maximum(low, x)
                    high_ = y if high_ is None else jnp.minimum(high_, y)
                bound_ref[top:stop, :] = jnp.where(line < LANES // 2, low, high_)
        for start, stop, at in link_spots:
            for tile in range(2):
                plain_ref[bank, 0, tile, unit + at : unit + at + stop - start, :] = (
                    FACE_SCALE
                    * jnp.minimum(
                        inline_ref[tile, start:stop, :], inline_ref[tile, start + 1 : stop + 1, :]
                    )
                )
        for kind in range(2):
            for tile in range(2):
                field_ref[bank, kind, tile * LANES : (tile + 1) * LANES, :] = jnp.transpose(
                    plain_ref[bank, kind, tile]
                )
        for y in range(0, chunk + SUB - 1, shifts):
            pieces = [
                field_ref[bank, 1, pl.ds(y + g * SUB, PITCH, stride=chunk), :]
                for g in range(GROUPS)
            ]
            block = jnp.transpose(jnp.concatenate(pieces, axis=0))
            for k in range(min(shifts, chunk + SUB - 1 - y)):
                for start, stop, at in cell_spots:
                    begin = k * unit + at
                    far_ref[pl.ds(start * deep + y + k, stop - start, stride=deep), :] = block[
                        begin : begin + stop - start
                    ]
        for c in range(0, chunk, 2):
            pieces = [
                field_ref[bank, 0, pl.ds(c + k, PITCH, stride=chunk), :]
                for k in range(min(2, chunk - c))
            ]
            piece = jnp.where(line < 3 * unit, pieces[0], roll(pieces[-1], 3 * unit))
            block = jnp.transpose(jnp.concatenate([piece] * GROUPS, axis=0))
            for k in range(len(pieces)):
                for kind, spots in enumerate((cell_spots, link_spots, cell_spots)):
                    for start, stop, at in spots:
                        begin = (3 * k + kind) * unit + at
                        face_ref[c + k, kind * high + start : kind * high + stop, :] = block[
                            begin : begin + stop - start
                        ]

    sub = lax.broadcasted_iota(jnp.int32, (SUB, LANES), 0)
    lane = lax.broadcasted_iota(jnp.int32, (SUB, LANES), 1)
    lag = ((lane // PITCH) * SUB + sub).astype(jnp.float32)
    key = jnp.where(lane < LANES // 2, lag, -lag)

    def build(t, carry):
        penalty = jnp.where(key < bound_ref[pl.ds(t, 1), :], PENALTY, 0.0)
        for c in range(chunk):
            near = face_ref[c, pl.ds(t, 1), :]
            diff = near - far_ref[pl.ds(t * deep + c, SUB), :]
            m_ref[t, c] = diff * diff + penalty
        return carry

    def weight(kind, c, t):
        return face_ref[c, pl.ds(kind * high + t, 1), :]

    def update(t, here, before, across):
        along = []
        for c in range(chunk):
            after = here[c + 1] if c < chunk - 1 else pltpu.roll(here[0], LANES - 1, 1)
            along.append(weight(2, c, t) * (after - here[c]))
        back = [pltpu.roll(along[-1], 1, 1)] + along[:-1]
        for c in range(chunk):
            m_ref[t, c] = (here[c] + (across[c] - before[c])) + (along[c] - back[c])

    def link(t, here, ahead):
        return [weight(1, c, t) * (ahead[c] - here[c]) for c in range(chunk)]

    def row(t):
        return [m_ref[t, c] for c in range(chunk)]

    def relax(t, state):
        here, before = state
        ahead = row(t + 1)
        across = link(t, here, ahead)
        update(t, here, before, across)
        return ahead, across

    def sweep(start, stop, before=None):
        here = row(start)
        if before is None:
            before = link(start - 1, row(start - 1), here)
        return lax.fori_loop(start, stop, relax, (here, before), unroll=stop - start)

    for dj in (-1, 1):
        arrive(0, dj)
    prepare(0, (0,), [(REACH, REACH + rows - 1)])
    lax.fori_loop(REACH, REACH + rows, build, 0, unroll=4)

    inner = min(3, (rows - 1) // 2)
    for step in range(1, min(inner, ITERS) + 1):
        start, stop = REACH + step, REACH + rows - step
        first = link(start - 1, row(start - 1), row(start))
        _, last_link = sweep(start, stop, first)
        for c in range(chunk):
            link_ref[0, step - 1, c] = first[c]
            link_ref[1, step - 1, c] = last_link[c]

    for di, dj in OFFSETS:
        if di:
            arrive(di, dj)
    prepare(1, (-1, 1), [(0, REACH), (REACH + rows - 1, tall - 1)])
    lax.fori_loop(0, REACH, build, 0, unroll=REACH)
    lax.fori_loop(REACH + rows, tall, build, 0, unroll=REACH)

    for step in range(1, ITERS):
        if step > inner:
            sweep(step, tall - step)
            continue
        edge_row = REACH + step - 1
        here, before = sweep(step, edge_row)
        update(edge_row, here, before, [link_ref[0, step - 1, c] for c in range(chunk)])
        first = [link_ref[1, step - 1, c] for c in range(chunk)]
        sweep(REACH + rows - step, tall - step, first)

    kept = range(REACH, REACH + rows)
    back = {}
    for t in kept:
        along = weight(2, chunk - 1, t) * (
            pltpu.roll(m_ref[t, 0], LANES - 1, 1) - m_ref[t, chunk - 1]
        )
        back[t] = (pltpu.roll(along, 1, 1), along)
    for c in range(chunk):
        here = m_ref[REACH, c]
        before = weight(1, c, REACH - 1) * (here - m_ref[REACH - 1, c])
        fresh = []
        for t in kept:
            ahead = m_ref[t + 1, c]
            across = weight(1, c, t) * (ahead - here)
            if c < chunk - 1:
                along = weight(2, c, t) * (m_ref[t, c + 1] - here)
            else:
                along = back[t][1]
            fresh.append((here + (across - before)) + (along - back[t][0]))
            back[t] = (along, back[t][1])
            here, before = ahead, across
        packed_ref[c * LANES : (c + 1) * LANES, :] = jnp.transpose(
            jnp.concatenate(fresh, axis=0)
        )

    def unpack(x):
        return [roll(x, -v) for v in range(GROUPS)]

    spots = [lane % GROUPS == v for v in range(GROUPS)]

    def pack(xs):
        result = xs[0]
        for v in range(1, GROUPS):
            result = jnp.where(spots[v], roll(xs[v], v), result)
        return result

    def loose(index):
        return pl.ds(pl.multiple_of(index * SUB, SUB), SUB)

    @pl.when(me > 0)
    def _():
        def loosen(i, carry):
            for c in range(chunk):
                x = packed_ref[pl.ds(c * LANES + i, SUB, stride=PITCH), :]
                for v, y in enumerate(unpack(x)):
                    loose_ref[loose((i * chunk + c) * GROUPS + v), :] = y
            return carry

        lax.fori_loop(REACH // chunk, (width + REACH - 1) // chunk + 1, loosen, 0)

    state_copy = pltpu.make_async_remote_copy(
        src_ref=leave_ref,
        dst_ref=enter_ref,
        send_sem=send_sem,
        recv_sem=recv_sem,
        device_id={"tm": lax.min(me + 1, count - 1)},
        device_id_type=pl.DeviceIdType.MESH,
    )

    at_low = sub == 0
    at_high = sub == SUB - 1
    top = GROUPS - 1
    wide3 = [jnp.full((SUB, LANES), strain_ref[k]) >= 3 for k in range(width // STRETCH)]
    wide2 = [jnp.full((SUB, LANES), strain_ref[k]) >= 2 for k in range(width // STRETCH)]

    def below(x):
        return jnp.where(at_low, BIG, pltpu.roll(x, 1, 0))

    def above(x):
        return jnp.where(at_high, BIG, pltpu.roll(x, SUB - 1, 0))

    def advance(x, cost, k):
        x = [below(x[top])] + x + [above(x[0])]
        pair = [jnp.minimum(x[v], x[v + 1]) for v in range(GROUPS + 1)]
        one = [jnp.minimum(pair[v], pair[v + 1]) for v in range(GROUPS)]
        wide = [below(one[top - 1]), below(one[top])] + one + [above(one[0]), above(one[1])]
        two = [jnp.minimum(wide[v], wide[v + 2]) for v in range(GROUPS + 2)]
        three = [jnp.minimum(two[v], two[v + 2]) for v in range(GROUPS)]
        result = []
        for v in range(GROUPS):
            near = jnp.where(wide2[k], two[v + 1], one[v])
            result.append(cost[v] + jnp.where(wide3[k], three[v], near))
        return result

    @pl.when(me == 0)
    def _():
        state = [jnp.zeros((SUB, LANES), jnp.float32)] * GROUPS
        for s in range(width):
            x = s + REACH
            cost = unpack(packed_ref[pl.ds((x % chunk) * LANES + x // chunk, SUB, stride=PITCH), :])
            state = advance(state, cost, s // STRETCH)
            for v in range(GROUPS):
                loose_ref[loose(s * GROUPS + v), :] = state[v]
        leave_ref[...] = pack(state)

    def follow(final):
        state_copy.wait_recv()
        state = unpack(enter_ref[...])
        for s in range(width):
            spots_s = [loose((s + REACH) * GROUPS + v) for v in range(GROUPS)]
            former = state
            state = advance(state, [loose_ref[spot, :] for spot in spots_s], s // STRETCH)
            if final and s:
                y_ref[(s - 1) * SUB : s * SUB, :] = pack(former)
            elif final:
                continue
            else:
                for v in range(GROUPS):
                    loose_ref[loose(s * GROUPS + v), :] = state[v]
        if final:
            y_ref[(width - 1) * SUB : width * SUB, :] = pack(state)
        else:
            leave_ref[...] = pack(state)

    @pl.when((me > 0) & (me < count - 1))
    def _():
        follow(False)

    @pl.when((me > 0) & (me == count - 1))
    def _():
        follow(True)

    @pl.when(me < count - 1)
    def _():
        state_copy.start()

    @pl.when(me < count - 1)
    def _():
        def tighten(s, carry):
            x = [loose_ref[loose(s * GROUPS + v), :] for v in range(GROUPS)]
            y_ref[pl.ds(pl.multiple_of(s * SUB, SUB), SUB), :] = pack(x)
            return carry

        lax.fori_loop(0, width, tighten, 0, unroll=16)

    @pl.when(me < count - 1)
    def _():
        state_copy.wait_send()

    for di, dj in OFFSETS:

        @pl.when(present(di, dj))
        def _():
            for copy in halo_copies(di, dj):
                copy.wait_send()


def spread(dims, y_ref, out_ref, ready_ref, sems):
    rows, width = dims
    blocks = [y_ref[pl.ds(g, width, stride=SUB), :] for g in range(SUB)]
    low = jnp.transpose(functools.reduce(jnp.minimum, blocks))
    least = [
        jnp.min(low[r * SUB : (r + 1) * SUB], axis=0, keepdims=True) for r in range(rows)
    ]
    copies = []
    for g in range(SUB):
        block = jnp.transpose(blocks[g])
        for r in range(rows):
            ready_ref[pl.ds(g * SUB * rows + r, SUB, stride=rows), :] = (
                block[r * SUB : (r + 1) * SUB] - least[r]
            )
        piece = pl.ds(g * SUB * rows, SUB * rows)
        copies.append(
            pltpu.make_async_copy(ready_ref.at[piece, :], out_ref.at[piece, :], sems.at[g])
        )
        copies[-1].start()
    for copy in copies:
        copy.wait()


def per_device(near_trace, far_trace, inline_weight, time_weight, lag_low, lag_high, strain):
    rows, width = near_trace.shape
    count = lax.axis_size("tm")
    count_in = lax.axis_size("inline")
    tall = rows + 2 * REACH
    high = -(-tall // SUB) * SUB
    chunk = -(-(width + 2 * REACH) // PITCH)
    deep = -(-(chunk + SUB - 1) // SUB) * SUB
    assert width == LANES and rows * SUB == LANES and SHIFTS * high <= LANES
    assert REACH + HALF + 3 * REACH < LANES - SUB and REACH <= rows
    assert chunk * PITCH + L <= 2 * LANES and REACH + HALF <= width
    vmem = pl.BlockSpec(memory_space=pltpu.VMEM)
    packed = pl.pallas_call(
        functools.partial(kernel, (rows, width, count, count_in, tall, high, chunk, deep)),
        out_shape=jax.ShapeDtypeStruct((width * SUB, LANES), jnp.float32),
        in_specs=[pl.BlockSpec(memory_space=pltpu.HBM)] * 7,
        out_specs=vmem,
        scratch_shapes=[
            pltpu.VMEM((2, rows, width), jnp.float32),
            pltpu.VMEM((2, rows, width), jnp.int32),
            pltpu.VMEM((2, rows, width), jnp.float32),
            pltpu.VMEM((2, 2, rows, width), jnp.float32),
            pltpu.VMEM((2, 2, rows, width), jnp.int32),
            pltpu.VMEM((9, rows, width), jnp.float32),
            pltpu.VMEM((2, 2, 2, LANES, LANES), jnp.float32),
            pltpu.VMEM((2, high, LANES), jnp.float32),
            pltpu.VMEM((2, 2, 2 * LANES, LANES), jnp.float32),
            pltpu.VMEM((chunk, LANES, LANES), jnp.float32),
            pltpu.VMEM((tall * deep, LANES), jnp.float32),
            pltpu.VMEM((high, LANES), jnp.float32),
            pltpu.VMEM((tall, chunk, SUB, LANES), jnp.float32),
            pltpu.VMEM((2, (rows - 1) // 2, chunk, SUB, LANES), jnp.float32),
            pltpu.VMEM((chunk * LANES, LANES), jnp.float32),
            pltpu.VMEM((chunk * PITCH * GROUPS * SUB, LANES), jnp.float32),
            pltpu.VMEM((SUB, LANES), jnp.float32),
            pltpu.VMEM((SUB, LANES), jnp.float32),
            pltpu.SMEM(lag_low.shape, jnp.int32),
            pltpu.SMEM(lag_high.shape, jnp.int32),
            pltpu.SMEM(strain.shape, jnp.int32),
            pltpu.SemaphoreType.DMA((7,)),
            pltpu.SemaphoreType.DMA((2, 9)),
            pltpu.SemaphoreType.DMA((2, 9)),
            pltpu.SemaphoreType.DMA,
            pltpu.SemaphoreType.DMA,
        ],
        compiler_params=pltpu.CompilerParams(
            collective_id=0, has_side_effects=True, vmem_limit_bytes=24 << 20
        ),
    )(
        *[
            pltpu.with_memory_space_constraint(x, pltpu.HBM)
            for x in (far_trace, near_trace, inline_weight, time_weight, lag_low, lag_high, strain)
        ]
    )
    out = pl.pallas_call(
        functools.partial(spread, (rows, width)),
        out_shape=jax.ShapeDtypeStruct((L * rows, width), jnp.float32),
        in_specs=[vmem],
        out_specs=pl.BlockSpec(memory_space=pltpu.HBM),
        scratch_shapes=[
            pltpu.VMEM((L * rows, width), jnp.float32),
            pltpu.SemaphoreType.DMA((SUB,)),
        ],
        compiler_params=pltpu.CompilerParams(vmem_limit_bytes=24 << 20),
    )(packed)
    return out.reshape(L, rows, width)


def solution(mesh):
    return jax.shard_map(
        per_device,
        mesh=mesh,
        in_specs=(
            P(("group", "inline"), "tm"),
            P(("group", "inline"), "tm"),
            P(("group", "inline"), "tm"),
            P(("group", "inline"), "tm"),
            P(("group", "inline")),
            P(("group", "inline")),
            P(("group", "tm")),
        ),
        out_specs=P(None, ("group", "inline"), "tm"),
        check_vma=False,
    )
```
